32 devices in a mesh: row: 8 (over z, core), col: 4 (over y, x).
Axes of the slice: x: 2, y: 2, z: 4, core: 2. Of those that a mesh axis runs over, the one named last changes fastest.
Arguments:
- inverse_factor: float32 [32, 1024, 1024], P(('row', 'col')), as said below
- coupling: float32 [32, 1024, 768], P(('row', 'col'))
- boundary_stiffness: float32 [32, 768, 768], P(('row', 'col')), as said below
- interior_mass: float32 [32, 1024], P(('row', 'col')), may hold values from 0.5 to 2
- boundary_mass: float32 [32, 768], P(('row', 'col')), may hold values from 0.5 to 1
- interface_ids: int32 [32, 768], replicated, may hold values from 0 to 8191, as said below
- trial_modes: float32 [8192, 512], P('col'), may hold values from -4 to 4
Outputs:
- reduced_matrix: float32 [8192, 8192], P('row', 'col')
- reduced_columns: float32 [512, 8192], P('col', 'row')
The draws below stay inside these ranges and needn't reach their ends.
Inputs may be any that keep to these rules, and one draw needn't show every extreme that they name: `interface_ids`: row s lists the 768 interface unknowns of substructure s as six distinct runs of 128 consecutive ids, each starting at a multiple of 128, runs in any order. With g = id // 128 the run's number, three runs of every list have g in one residue class modulo 2, the same class for all lists, and the other three are spread evenly over the other classes; every run number is listed by some substructure. `inverse_factor`: lower triangular with a positive diagonal. Symmetric, and boundary_stiffness[s] - W_s^T W_s is positive definite.
All inputs are finite; a program needn't handle non-finite values.
Results may differ from the reference program's by a relative error of at most 0.0001.
Values sent between devices are 32-bit elements; how exact they have to be, the bound alone decides.
No kernel may reach another device: no remote copies, remote signals or barrier semaphores. Data moves between devices by JAX's collectives and lax.ppermute only.
A program may use at most 192 MiB of HBM per device.

```python
import math
import jax
import jax.numpy as jnp
from jax import lax

NI = 1024
IDB = 128
SUB = 32
NB = 768
NG = 8192
MODES = 512
PANEL = 512
SUBS = 32
N_ROW = 8
N_COL = 4


def substructure(key, index):
    sub_key = jax.random.fold_in(jax.random.fold_in(key, 77), index)
    keys = jax.random.split(sub_key, 6)
    diag_part = jnp.exp(jax.random.uniform(keys[0], (NI,), jnp.float32, jnp.log(0.5), jnp.log(1.5)))
    strict = jnp.tril(jax.random.normal(keys[1], (NI, NI), jnp.float32), -1) * (0.5 / NI ** 0.5)
    factor = jnp.diag(diag_part) + strict
    link = jax.random.normal(keys[2], (NI, NB), jnp.float32) * 0.01
    weighted = jnp.dot(factor, link, precision=lax.Precision.HIGHEST)
    random_base = jax.random.normal(keys[4], (NB, NB), jnp.float32)
    dominant = jax.random.uniform(keys[5], (NB,), jnp.float32, 0.5, 1.0)
    stiff = jnp.dot(weighted.T, weighted, precision=lax.Precision.HIGHEST) + jnp.diag(dominant)
    stiff = stiff + 0.3 * jnp.dot(random_base, random_base.T, precision=lax.Precision.HIGHEST) / NB
    stiff = 0.5 * (stiff + stiff.T)
    return (factor, link, stiff)


def draw_everything(key):
    return lax.map(lambda index: substructure(key, index), jnp.arange(N_ROW * N_COL))


def draw_inverse_factor(key, part):
    return draw_everything(key)[0]


def draw_coupling(key, part):
    return draw_everything(key)[1]


def draw_boundary_stiffness(key, part):
    return draw_everything(key)[2]


def draw_interface_ids(key, part):
    total_subs = N_ROW * N_COL
    classes = N_ROW // 4
    per_class = NG // IDB // classes
    spread = 3 // (classes - 1)
    base_key = jax.random.fold_in(key, 5)
    heavy_class = jax.random.randint(jax.random.fold_in(base_key, 1), (), 0, classes)
    offsets = jax.random.permutation(jax.random.fold_in(base_key, 2), total_subs) % per_class
    groups = [(offsets + shift_count) % per_class * classes + heavy_class for shift_count in range(3)]
    for remaining in range(1, classes):
        other_offsets = jax.random.permutation(jax.random.fold_in(base_key, 10 + remaining), total_subs) % per_class
        class_index = (heavy_class + remaining) % classes
        for shift_count in range(spread):
            groups.append((other_offsets + shift_count) % per_class * classes + class_index)
    blocks = jnp.stack(groups, axis=1).astype(jnp.int32)
    order_keys = jax.random.split(jax.random.fold_in(base_key, 3), total_subs)
    orders = jax.vmap(lambda row_key: jax.random.permutation(row_key, 6))(order_keys)
    blocks = jnp.take_along_axis(blocks, orders, axis=1)
    id_values = blocks[:, :, None] * IDB + jnp.arange(IDB, dtype=jnp.int32)[None, None, :]
    return id_values.reshape(total_subs, NB).astype(jnp.int32)


def level_of(stream_key, shape, cuts, smallest, high):
    def one(position, blocks):
        steps = jax.random.uniform(jax.random.fold_in(jax.random.fold_in(stream_key, 6), position), (blocks,), jnp.float32, smallest / len(cuts), high / len(cuts))
        return jnp.repeat(jnp.exp(steps), shape[position] // blocks).reshape((-1,) + (1,) * (len(shape) - position - 1))

    gain = one(*cuts[0])
    for cut in cuts[1:]:
        gain = gain * one(*cut)
    return gain


def gaussian(key, extent, scale, bound, cuts=(), held_as=jnp.bfloat16):
    gain = level_of(key, extent, cuts, -0.22, 0.18) if cuts else 1.0
    array = jax.random.normal(key, extent, jnp.float32) * scale * gain
    return jnp.minimum(jnp.maximum(array, -bound), bound).astype(held_as)


def setup_inputs(seed: int = 0) -> dict:
    key_list = jax.random.split(jax.random.key(seed), 8)
    return {
        "inverse_factor": draw_inverse_factor(jax.random.fold_in(key_list[7], 71), 0),
        "coupling": draw_coupling(jax.random.fold_in(key_list[7], 71), 0),
        "boundary_stiffness": draw_boundary_stiffness(jax.random.fold_in(key_list[7], 71), 0),
        "interior_mass": jnp.clip(jnp.exp(math.log(2.0) - 1.3862944 * jax.random.uniform(key_list[3], (SUBS, NI), jnp.float32) ** level_of(key_list[3], (SUBS, NI), ((0, 32),), -0.2, 0.2)), 0.5, 2.0),
        "boundary_mass": jnp.clip(jnp.exp(math.log(1.0) - 0.6931472 * jax.random.uniform(key_list[4], (SUBS, NB), jnp.float32) ** level_of(key_list[4], (SUBS, NB), ((0, 32),), -0.2, 0.2)), 0.5, 1.0),
        "interface_ids": draw_interface_ids(jax.random.fold_in(key_list[7], 71), 0),
        "trial_modes": gaussian(key_list[6], (NG, MODES), 0.3, 4.0, ((0, 4),), jnp.float32),
    }


highest = lax.Precision.HIGHEST
shift_value = 0.05

def lower_solve(lower, rhs):
    return lax.linalg.triangular_solve(lower, rhs, left_side=True, lower=True)

def condense(factor, link, stiff, inner_mass, outer_mass):
    weighted = jnp.dot(factor, link, precision=highest)
    condensed_k = stiff - jnp.dot(weighted.T, weighted, precision=highest)
    static = jnp.dot(factor.T, weighted, precision=highest)
    condensed_m = jnp.diag(outer_mass) + jnp.dot(static.T, inner_mass[:, None] * static, precision=highest)
    return (condensed_k, condensed_m)

def reference(inverse_factor, coupling, boundary_stiffness, interior_mass, boundary_mass, interface_ids, trial_modes):

    def assemble(carry, items):
        stiff_all, mass_all = carry
        factor, link, stiff, inner_mass, outer_mass, id_values = items
        condensed_k, condensed_m = condense(factor, link, stiff, inner_mass, outer_mass)
        stiff_all = stiff_all.at[id_values[:, None], id_values[None, :]].add(condensed_k)
        mass_all = mass_all.at[id_values[:, None], id_values[None, :]].add(condensed_m)
        return ((stiff_all, mass_all), None)
    zero_matrix = jnp.zeros((NG, NG), jnp.float32)
    (stiff_all, mass_all), _ = lax.scan(assemble, (zero_matrix, zero_matrix), (inverse_factor, coupling, boundary_stiffness, interior_mass, boundary_mass, interface_ids))
    shifted = stiff_all - shift_value * mass_all
    row_blocks = NG // (SUB * N_ROW)
    col_blocks = NG // (SUB * N_COL)
    modes = trial_modes.reshape(N_COL, col_blocks, SUB, MODES).transpose(1, 0, 2, 3).reshape(NG, MODES)
    products = jnp.dot(mass_all, modes, precision=highest)
    lower = jnp.linalg.cholesky(shifted[:PANEL, :PANEL])
    left_solved = lower_solve(lower, shifted[:, :PANEL].T)
    right_solved = lower_solve(lower, shifted[:PANEL, :])
    modes_solved = lower_solve(lower, products[:PANEL, :])
    reduced = shifted - jnp.dot(left_solved.T, right_solved, precision=highest)
    columns = products - jnp.dot(left_solved.T, modes_solved, precision=highest)
    reduced = reduced.reshape(row_blocks, N_ROW, SUB, col_blocks, N_COL, SUB).transpose(1, 0, 2, 4, 3, 5).reshape(NG, NG)
    columns = columns.reshape(row_blocks, N_ROW, SUB, MODES).transpose(3, 1, 0, 2).reshape(MODES, NG)
    return (reduced, columns)
```

```python
import functools
import jax
import jax.numpy as jnp
from jax import lax
from jax.experimental import pallas as pl
from jax.experimental.pallas import tpu as pltpu
from jax.sharding import PartitionSpec as P

IDB = 128
SUB = 32
NG = 8192
PANEL = 512
PER_RUN = IDB // SUB
LANES = 128
SUBLANES = 8
GROUPS = SUB // SUBLANES

highest = lax.Precision.HIGHEST
high = lax.Precision.HIGH
shift_value = 0.05
VMEM_LIMIT = 60 * 1024 * 1024


def tdot(left, right, precision):
    return lax.dot_general(left, right, (((0,), (0,)), ((), ())), precision=precision)


class Grid:
    def __init__(self, row_count, col_count):
        self.rows = row_count
        self.cols = col_count
        self.devices = row_count * col_count
        self.row_classes = row_count // PER_RUN
        self.col_classes = col_count // PER_RUN
        self.row_cap = 3
        self.col_cap = 3 + (self.row_classes // self.col_classes - 1) * (3 // (self.row_classes - 1))
        self.slots = self.row_cap * self.col_cap


def call(kernel, out_shape, in_specs, scratch=(), flops=0, nbytes=0):
    return pl.pallas_call(
        kernel,
        out_shape=out_shape,
        in_specs=in_specs,
        out_specs=jax.tree.map(lambda _: pl.BlockSpec(memory_space=pltpu.VMEM), out_shape),
        scratch_shapes=list(scratch),
        compiler_params=pltpu.CompilerParams(vmem_limit_bytes=VMEM_LIMIT),
        cost_estimate=pl.CostEstimate(flops=flops, bytes_accessed=nbytes, transcendentals=0),
    )


SMEM = pl.BlockSpec(memory_space=pltpu.SMEM)
VMEM = pl.BlockSpec(memory_space=pltpu.VMEM)


def ranks_of(groups, classes):
    kinds = [g % classes for g in groups]
    ranks = []
    for j in range(len(kinds)):
        rank = jnp.int32(0)
        for i in range(j):
            rank = rank + jnp.where(kinds[i] == kinds[j], 1, 0).astype(jnp.int32)
        ranks.append(rank)
    return kinds, ranks


def lane_group():
    return lax.broadcasted_iota(jnp.int32, (SUBLANES, LANES), 1) // SUB


def regroup(tile):
    parts = [tile[SUBLANES * q : SUBLANES * (q + 1)] for q in range(GROUPS)]
    where = lane_group()
    out = []
    for k in range(PER_RUN):
        value = None
        for q in range(GROUPS):
            turn = (q - k) % PER_RUN * SUB
            piece = parts[q] if turn == 0 else pltpu.roll(parts[q], turn, 1)
            value = piece if value is None else jnp.where(where == q, piece, value)
        out.append(value)
    return out


def pack_matrix(grid, runs_ref, own_ref, a_ref, out_ref):
    number = a_ref.shape[0] // IDB
    groups = [runs_ref[own_ref[0], j] for j in range(number)]
    row_kind, row_rank = ranks_of(groups, grid.row_classes)
    col_kind, col_rank = ranks_of(groups, grid.col_classes)
    if grid.devices * grid.slots != (number * PER_RUN) ** 2:
        out_ref[...] = jnp.zeros_like(out_ref)
    for i in range(number):
        for k in range(PER_RUN):
            for j in range(number):
                tile = a_ref[i * IDB + k * SUB : i * IDB + (k + 1) * SUB, j * IDB : (j + 1) * IDB]
                row = (row_kind[i] * PER_RUN + k) * grid.cols
                slot = row_rank[i] * grid.col_cap + col_rank[j]
                for kk, value in enumerate(regroup(tile)):
                    out_ref[row + col_kind[j] * PER_RUN + kk, slot] = value


def pack_modes(grid, per_device, runs_ref, own_ref, y_ref, out_ref):
    number = y_ref.shape[1] // IDB
    groups = [runs_ref[own_ref[0], j] for j in range(number)]
    row_kind, row_rank = ranks_of(groups, grid.row_classes)
    if grid.devices * grid.row_cap != number * PER_RUN * grid.cols:
        out_ref[...] = jnp.zeros_like(out_ref)
    for m in range(y_ref.shape[0] // SUB):
        for j in range(number):
            tile = y_ref[m * SUB : (m + 1) * SUB, j * IDB : (j + 1) * IDB]
            slot = row_rank[j] * per_device + m % per_device
            for k, value in enumerate(regroup(tile)):
                row = (row_kind[j] * PER_RUN + k) * grid.cols + m // per_device
                out_ref[row, slot] = value


def list_places(runs_ref, source, number, classes, kind, cap, table_ref):
    count = jnp.int32(0)
    for j in range(number):
        g = runs_ref[source, j]
        table_ref[source, count] = g // classes
        count = count + jnp.where(g % classes == kind, 1, 0).astype(jnp.int32)
    for t in range(cap):
        table_ref[source, t] = jnp.where(t < count, table_ref[source, t], -1)


def add_block(acc_ref, row, place, value):
    valid = place >= 0
    place = jnp.maximum(place, 0)
    turn = place % PER_RUN
    start = pl.multiple_of(place // PER_RUN * LANES, LANES)
    mask = (lane_group() == turn) & valid
    parts = []
    for q in range(GROUPS):
        moved = pltpu.roll(value, (turn - q + PER_RUN) % PER_RUN * SUB, 1)
        parts.append(jnp.where(mask, moved, 0.0))
    acc_ref[pl.ds(row, SUB), pl.ds(start, LANES)] += jnp.concatenate(parts, axis=0)


def place_matrix(grid, runs_ref, own_ref, in_ref, acc_ref, row_tab, col_tab):
    sources, number = runs_ref.shape
    row_kind = own_ref[0] // grid.cols // PER_RUN
    col_kind = own_ref[0] % grid.cols // PER_RUN
    acc_ref[...] = jnp.zeros_like(acc_ref)

    @pl.loop(0, sources)
    def _(s):
        list_places(runs_ref, s, number, grid.row_classes, row_kind, grid.row_cap, row_tab)
        list_places(runs_ref, s, number, grid.col_classes, col_kind, grid.col_cap, col_tab)

    @pl.loop(0, sources)
    def _(s):
        for t in range(grid.row_cap):
            row_place = row_tab[s, t]
            row = pl.multiple_of(jnp.maximum(row_place, 0) * SUB, SUB)
            for u in range(grid.col_cap):
                place = jnp.where(row_place >= 0, col_tab[s, u], -1)
                add_block(acc_ref, row, place, in_ref[s, t * grid.col_cap + u])


def place_modes(grid, per_device, runs_ref, own_ref, in_ref, acc_ref, row_tab):
    sources, number = runs_ref.shape
    row_kind = own_ref[0] // grid.cols // PER_RUN
    acc_ref[...] = jnp.zeros_like(acc_ref)

    @pl.loop(0, sources)
    def _(s):
        list_places(runs_ref, s, number, grid.row_classes, row_kind, grid.row_cap, row_tab)

    @pl.loop(0, sources)
    def _(s):
        for t in range(grid.row_cap):
            place = row_tab[s, t]
            for m in range(per_device):
                add_block(acc_ref, m * SUB, place, in_ref[s, t * per_device + m])


def pick_modes(grid, runs_ref, own_ref, modes_ref, out_ref):
    number = runs_ref.shape[1]
    own_row = own_ref[0] // grid.cols
    col_kind = own_ref[0] % grid.cols // PER_RUN
    if grid.cols * grid.col_cap != number * PER_RUN:
        out_ref[...] = jnp.zeros_like(out_ref)
    for c in range(grid.cols):
        groups = [runs_ref[own_row * grid.cols + c, j] for j in range(number)]
        kinds, ranks = ranks_of(groups, grid.col_classes)
        for j in range(number):

            @pl.when(kinds[j] == col_kind)
            def _():
                row = pl.multiple_of(groups[j] // grid.col_classes * SUB, SUB)
                out_ref[c, ranks[j]] = modes_ref[pl.ds(row, SUB), :]


def order_modes(grid, runs_ref, own_ref, in_ref, out_ref):
    number = runs_ref.shape[1]
    groups = [runs_ref[own_ref[0], j] for j in range(number)]
    kinds, ranks = ranks_of(groups, grid.col_classes)
    for j in range(number):
        for k in range(PER_RUN):
            start = j * IDB + k * SUB
            out_ref[start : start + SUB, :] = in_ref[kinds[j] * PER_RUN + k, ranks[j]]


def invert_block(matrix):
    n = matrix.shape[0]
    count = n // SUBLANES
    sub = lax.broadcasted_iota(jnp.int32, (SUBLANES, n), 0)
    lane = lax.broadcasted_iota(jnp.int32, (SUBLANES, n), 1)

    def across(value, m):
        return jnp.broadcast_to(value[:, m : m + 1], (SUBLANES, n))

    def down(value, k):
        return jnp.broadcast_to(value[k : k + 1, :], (SUBLANES, n))

    def panel(_, rows):
        head = rows[0]
        split = [across(head, m) for m in range(SUBLANES)]
        for k in range(SUBLANES):
            inverse = 1.0 / down(split[k], k)
            mine = sub == k
            head = jnp.where(lane == k, jnp.where(mine, 1.0, 0.0), head)
            pivot = down(head, k) * inverse
            factor = split[k]
            head = jnp.where(mine, pivot, head - factor * pivot)
            for m in range(k + 1, SUBLANES):
                scaled = down(split[m], k) * inverse
                split[m] = jnp.where(mine, scaled, split[m] - factor * scaled)
        lines = [down(head, m) for m in range(SUBLANES)]
        done = []
        for row in rows[1:]:
            value = jnp.where(lane < SUBLANES, 0.0, row)
            for m in range(SUBLANES):
                value = value - across(row, m) * lines[m]
            done.append(value)
        done.append(head)
        return tuple(pltpu.roll(value, n - SUBLANES, 1) for value in done)

    rows = tuple(matrix[SUBLANES * i : SUBLANES * (i + 1)] for i in range(count))
    rows = lax.fori_loop(0, count, panel, rows)
    return jnp.concatenate(rows, axis=0)


def invert_corner(grid, pieces_ref, out_ref, work_ref):
    row_blocks = PANEL // SUB // grid.rows
    col_blocks = PANEL // SUB // grid.cols
    width = col_blocks * SUB

    def col_position(block):
        return (block % grid.cols) * col_blocks + block // grid.cols

    for r in range(grid.rows):
        for b in range(row_blocks):
            start = col_position(r + grid.rows * b) * SUB
            for c in range(grid.cols):
                work_ref[start : start + SUB, c * width : (c + 1) * width] = pieces_ref[
                    r * grid.cols + c, b * SUB : (b + 1) * SUB, :
                ]
    steps = PANEL // LANES
    lane = lax.broadcasted_iota(jnp.int32, (LANES, PANEL), 1) // LANES

    @pl.loop(0, steps)
    def _(step):
        at = pl.ds(pl.multiple_of(step * LANES, LANES), LANES)
        small = invert_block(work_ref[at, at])
        line = jnp.dot(small, work_ref[at, :], precision=highest, preferred_element_type=jnp.float32)
        line = jnp.where(lane == step, jnp.concatenate([small] * steps, axis=1), line)
        for i in range(steps):
            rows = slice(i * LANES, (i + 1) * LANES)
            factor = work_ref[rows, at]
            kept = jnp.where(lane == step, 0.0, work_ref[rows, :])
            update = kept - jnp.dot(
                factor, line, precision=highest, preferred_element_type=jnp.float32
            )
            work_ref[rows, :] = jnp.where(i == step, line, update)

    for r in range(grid.rows):
        for b in range(row_blocks):
            source = col_position(r + grid.rows * b) * SUB
            target = (r * row_blocks + b) * SUB
            out_ref[target : target + SUB, :] = work_ref[source : source + SUB, :]


def spread(value, axis, count):
    copies = jnp.broadcast_to(value[None], (count,) + value.shape)
    return lax.all_to_all(copies, axis, 0, 0, tiled=True)


def body(
    inverse_factor,
    coupling,
    boundary_stiffness,
    interior_mass,
    boundary_mass,
    interface_ids,
    trial_modes,
):
    grid = Grid(lax.axis_size("row"), lax.axis_size("col"))
    f32 = jnp.float32
    modes = trial_modes.shape[1]
    mode_count = modes // grid.cols
    per_device = mode_count // SUB
    size = coupling.shape[2]
    sources = interface_ids.shape[0]
    local_rows = NG // grid.rows
    local_cols = NG // grid.cols
    runs = interface_ids[:, ::IDB] // IDB
    own = (lax.axis_index("row") * grid.cols + lax.axis_index("col")).astype(jnp.int32).reshape(1)

    wanted = call(
        functools.partial(pick_modes, grid),
        jax.ShapeDtypeStruct((grid.cols, grid.col_cap, SUB, modes), f32),
        [SMEM, SMEM, VMEM],
        nbytes=trial_modes.size * 8,
    )(runs, own, trial_modes)
    wanted = lax.all_to_all(wanted, "col", 0, 0, tiled=True)

    factor = inverse_factor[0]
    weighted = jnp.dot(factor, coupling[0], precision=high)
    static = tdot(factor, weighted, high)
    condensed_m = jnp.diag(boundary_mass[0]) + tdot(static, interior_mass[0][:, None] * static, high)
    shifted_s = boundary_stiffness[0] - tdot(weighted, weighted, high) - shift_value * condensed_m

    outbox = call(
        functools.partial(pack_matrix, grid),
        jax.ShapeDtypeStruct((grid.devices, grid.slots, SUBLANES, LANES), f32),
        [SMEM, SMEM, VMEM],
        nbytes=size * size * 8,
    )(runs, own, shifted_s)
    inbox = lax.all_to_all(outbox, ("row", "col"), 0, 0, tiled=True)

    own_modes = call(
        functools.partial(order_modes, grid),
        jax.ShapeDtypeStruct((size, modes), f32),
        [SMEM, SMEM, VMEM],
        nbytes=size * modes * 8,
    )(runs, own, wanted)
    weighted_modes = tdot(own_modes, condensed_m, high)
    mode_outbox = call(
        functools.partial(pack_modes, grid, per_device),
        jax.ShapeDtypeStruct((grid.devices, grid.row_cap * per_device, SUBLANES, LANES), f32),
        [SMEM, SMEM, VMEM],
        nbytes=size * modes * 8,
    )(runs, own, weighted_modes)
    mode_outbox, inbox = lax.optimization_barrier((mode_outbox, inbox))
    mode_inbox = lax.all_to_all(mode_outbox, ("row", "col"), 0, 0, tiled=True)

    shifted = call(
        functools.partial(place_matrix, grid),
        jax.ShapeDtypeStruct((local_rows, local_cols), f32),
        [SMEM, SMEM, VMEM],
        [
            pltpu.SMEM((sources, size // IDB + 1), jnp.int32),
            pltpu.SMEM((sources, size // IDB + 1), jnp.int32),
        ],
        nbytes=local_rows * local_cols * 8,
    )(runs, own, inbox)

    panel_row_count = PANEL // grid.rows
    panel_col_count = PANEL // grid.cols
    pieces = spread(shifted[:panel_row_count, :panel_col_count], ("row", "col"), grid.devices)
    panel_cols = spread(shifted[:, :panel_col_count], "col", grid.cols)
    panel_cols = panel_cols.transpose(1, 0, 2).reshape(local_rows, PANEL)
    panel_rows = lax.all_gather(shifted[:panel_row_count, :], "row", axis=0, tiled=True)

    inverse = call(
        functools.partial(invert_corner, grid),
        jax.ShapeDtypeStruct((PANEL, PANEL), f32),
        [VMEM],
        [pltpu.VMEM((PANEL, PANEL), f32)],
        flops=4 * PANEL**3,
        nbytes=PANEL * PANEL * 80,
    )(pieces)

    solved = lax.dot_general(inverse, panel_cols, (((1,), (1,)), ((), ())), precision=highest)
    reduced_matrix = shifted - tdot(solved, panel_rows, high)

    modes_local = call(
        functools.partial(place_modes, grid, per_device),
        jax.ShapeDtypeStruct((mode_count, local_rows), f32),
        [SMEM, SMEM, VMEM],
        [pltpu.SMEM((sources, size // IDB + 1), jnp.int32)],
        nbytes=mode_count * local_rows * 8,
    )(runs, own, mode_inbox)
    panel_modes = spread(modes_local[:, :panel_row_count].T, "row", grid.rows).reshape(PANEL, -1)
    reduced_columns = modes_local - tdot(panel_modes, solved, high)
    return (reduced_matrix, reduced_columns)


def solution(mesh):
    return jax.shard_map(
        body,
        mesh=mesh,
        in_specs=(
            P(("row", "col"), None, None),
            P(("row", "col"), None, None),
            P(("row", "col"), None, None),
            P(("row", "col"), None),
            P(("row", "col"), None),
            P(),
            P("col", None),
        ),
        out_specs=(P("row", "col"), P("col", "row")),
        check_vma=False,
    )
```

```python
import functools
import jax
import jax.numpy as jnp
from jax import lax
from jax.experimental import pallas as pl
from jax.experimental.pallas import tpu as pltpu
from jax.sharding import PartitionSpec as P

IDB = 128
SUB = 32
NG = 8192
PANEL = 512
PER_RUN = IDB // SUB
LANES = 128
SUBLANES = 8
GROUPS = SUB // SUBLANES

highest = lax.Precision.HIGHEST
high = lax.Precision.HIGH
shift_value = 0.05
VMEM_LIMIT = 60 * 1024 * 1024


def tdot(left, right, precision):
    return lax.dot_general(left, right, (((0,), (0,)), ((), ())), precision=precision)


class Grid:
    def __init__(self, row_count, col_count):
        self.rows = row_count
        self.cols = col_count
        self.devices = row_count * col_count
        self.row_classes = row_count // PER_RUN
        self.col_classes = col_count // PER_RUN
        self.row_cap = 3
        self.col_cap = 3 + (self.row_classes // self.col_classes - 1) * (3 // (self.row_classes - 1))
        self.slots = self.row_cap * self.col_cap
        evens = list(range(0, row_count, 2))
        halves = [evens[: len(evens) // 2], evens[len(evens) // 2 :]]
        self.order = [e + core for half in halves for core in range(2) for e in half]


def call(kernel, out_shape, in_specs, scratch=(), flops=0, nbytes=0):
    return pl.pallas_call(
        kernel,
        out_shape=out_shape,
        in_specs=in_specs,
        out_specs=jax.tree.map(lambda _: pl.BlockSpec(memory_space=pltpu.VMEM), out_shape),
        scratch_shapes=list(scratch),
        compiler_params=pltpu.CompilerParams(vmem_limit_bytes=VMEM_LIMIT),
        cost_estimate=pl.CostEstimate(flops=flops, bytes_accessed=nbytes, transcendentals=0),
    )


SMEM = pl.BlockSpec(memory_space=pltpu.SMEM)
VMEM = pl.BlockSpec(memory_space=pltpu.VMEM)


def ranks_of(groups, classes):
    kinds = [g % classes for g in groups]
    ranks = []
    for j in range(len(kinds)):
        rank = jnp.int32(0)
        for i in range(j):
            rank = rank + jnp.where(kinds[i] == kinds[j], 1, 0).astype(jnp.int32)
        ranks.append(rank)
    return kinds, ranks


def lane_group():
    return lax.broadcasted_iota(jnp.int32, (SUBLANES, LANES), 1) // SUB


def regroup(ref, row, lanes, turn):
    parts = []
    for g in range(GROUPS):
        start = row + (g - turn + GROUPS) % GROUPS * SUBLANES
        parts.append(ref[pl.ds(pl.multiple_of(start, SUBLANES), SUBLANES), lanes])
    where = lane_group()
    out = []
    for k in range(PER_RUN):
        value = None
        for g in range(GROUPS):
            shift = (g - k) % PER_RUN * SUB
            piece = parts[g] if shift == 0 else pltpu.roll(parts[g], shift, 1)
            value = piece if value is None else jnp.where(where == g, piece, value)
        out.append(value)
    return out


def pack_matrix(grid, runs_ref, own_ref, a_ref, out_ref):
    number = a_ref.shape[0] // IDB
    groups = [runs_ref[own_ref[0], j] for j in range(number)]
    row_kind, row_rank = ranks_of(groups, grid.row_classes)
    col_kind, col_rank = ranks_of(groups, grid.col_classes)
    turn = [g // grid.col_classes % PER_RUN for g in groups]
    if grid.devices * grid.slots != (number * PER_RUN) ** 2:
        out_ref[...] = jnp.zeros_like(out_ref)
    for i in range(number):
        for k in range(PER_RUN):
            for j in range(number):
                lanes = slice(j * IDB, (j + 1) * IDB)
                row = (row_kind[i] * PER_RUN + k) * grid.cols
                slot = row_rank[i] * grid.col_cap + col_rank[j]
                for kk, value in enumerate(regroup(a_ref, i * IDB + k * SUB, lanes, turn[j])):
                    out_ref[row + col_kind[j] * PER_RUN + kk, slot] = value


def pack_modes(grid, per_device, runs_ref, own_ref, y_ref, out_ref):
    number = y_ref.shape[1] // IDB
    groups = [runs_ref[own_ref[0], j] for j in range(number)]
    row_kind, row_rank = ranks_of(groups, grid.row_classes)
    turn = [g // grid.row_classes % PER_RUN for g in groups]
    if grid.devices * grid.row_cap != number * PER_RUN * grid.cols:
        out_ref[...] = jnp.zeros_like(out_ref)
    for m in range(y_ref.shape[0] // SUB):
        for j in range(number):
            lanes = slice(j * IDB, (j + 1) * IDB)
            slot = row_rank[j] * per_device + m % per_device
            for k, value in enumerate(regroup(y_ref, m * SUB, lanes, turn[j])):
                row = (row_kind[j] * PER_RUN + k) * grid.cols + m // per_device
                out_ref[row, slot] = value


def list_places(runs, classes, kind, cap):
    mine = (runs % classes == kind).astype(jnp.int32)
    number = runs.shape[1]
    earlier = jnp.arange(number)[:, None] < jnp.arange(number)[None, :]
    rank = jnp.sum(jnp.where(earlier[None], mine[:, :, None], 0), axis=1)
    hit = (mine[:, :, None] == 1) & (rank[:, :, None] == jnp.arange(cap)[None, None, :])
    return jnp.sum(jnp.where(hit, runs[:, :, None] // classes + 1, 0), axis=1) - 1


def add_blocks(acc_ref, blocks):
    where = lane_group()
    todo = []
    for row, place, value in blocks:
        valid = place >= 0
        place = jnp.maximum(place, 0)
        start = pl.multiple_of(place // PER_RUN * LANES, LANES)
        mask = (where == place % PER_RUN) & valid
        for q in range(GROUPS):
            moved = value if q == 0 else pltpu.roll(value, LANES - q * SUB, 1)
            at = (pl.ds(row + q * SUBLANES, SUBLANES), pl.ds(start, LANES))
            todo.append((at, acc_ref[at] + moved, mask))
    for at, value, mask in todo:
        pltpu.store(acc_ref.at[at], value, mask=mask)


def place_matrix(grid, row_tab, col_tab, in_ref, acc_ref):
    acc_ref[...] = jnp.zeros_like(acc_ref)

    @pl.loop(0, row_tab.shape[0])
    def _(s):
        blocks = []
        for t in range(grid.row_cap):
            row_place = row_tab[s, t]
            row = pl.multiple_of(jnp.maximum(row_place, 0) * SUB, SUB)
            for u in range(grid.col_cap):
                place = jnp.where(row_place >= 0, col_tab[s, u], -1)
                blocks.append((row, place, in_ref[s, t * grid.col_cap + u]))
        add_blocks(acc_ref, blocks)


def place_panel(grid, row_tab, col_tab, in_ref, rows_ref, cols_ref, corner_ref):
    row_limit = rows_ref.shape[0] // SUB
    col_limit = cols_ref.shape[1] // SUB
    rows_ref[...] = jnp.zeros_like(rows_ref)
    cols_ref[...] = jnp.zeros_like(cols_ref)

    @pl.loop(0, row_tab.shape[0])
    def _(s):
        def row_of(t):
            return pl.multiple_of(jnp.maximum(row_tab[s, t], 0) * SUB, SUB)

        for t in range(grid.row_cap):

            @pl.when((row_tab[s, t] >= 0) & (row_tab[s, t] < row_limit))
            def _():
                add_blocks(
                    rows_ref,
                    [(row_of(t), col_tab[s, u], in_ref[s, t * grid.col_cap + u]) for u in range(grid.col_cap)],
                )

        for u in range(grid.col_cap):

            @pl.when((col_tab[s, u] >= 0) & (col_tab[s, u] < col_limit))
            def _():
                add_blocks(
                    cols_ref,
                    [
                        (row_of(t), jnp.where(row_tab[s, t] >= 0, col_tab[s, u], -1), in_ref[s, t * grid.col_cap + u])
                        for t in range(grid.row_cap)
                    ],
                )

    corner_ref[...] = cols_ref[: row_limit * SUB, : col_limit * SUB]


def place_modes(grid, per_device, row_tab, in_ref, acc_ref):
    acc_ref[...] = jnp.zeros_like(acc_ref)

    @pl.loop(0, row_tab.shape[0])
    def _(s):
        blocks = []
        for t in range(grid.row_cap):
            place = row_tab[s, t]
            blocks += [(m * SUB, place, in_ref[s, t * per_device + m]) for m in range(per_device)]
        add_blocks(acc_ref, blocks)


def pick_modes(grid, runs_ref, own_ref, modes_ref, out_ref):
    number = runs_ref.shape[1]
    own_row = own_ref[0] // grid.cols
    own_col = own_ref[0] % grid.cols
    col_kind = own_col // PER_RUN
    if grid.cols * grid.col_cap != number * PER_RUN:
        out_ref[...] = jnp.zeros_like(out_ref)
    for c in range(grid.cols):
        groups = [runs_ref[own_row * grid.cols + (own_col ^ c), j] for j in range(number)]
        kinds, ranks = ranks_of(groups, grid.col_classes)
        for j in range(number):

            @pl.when(kinds[j] == col_kind)
            def _():
                row = pl.multiple_of(groups[j] // grid.col_classes * SUB, SUB)
                out_ref[c, ranks[j]] = modes_ref[pl.ds(row, SUB), :]


def order_modes(grid, runs_ref, own_ref, in_ref, out_ref):
    own_col = own_ref[0] % grid.cols
    number = runs_ref.shape[1]
    groups = [runs_ref[own_ref[0], j] for j in range(number)]
    kinds, ranks = ranks_of(groups, grid.col_classes)
    for j in range(number):
        for k in range(PER_RUN):
            start = j * IDB + k * SUB
            out_ref[start : start + SUB, :] = in_ref[(kinds[j] * PER_RUN + k) ^ own_col, ranks[j]]


def invert_block(matrix):
    n = matrix.shape[0]
    count = n // SUBLANES
    sub = lax.broadcasted_iota(jnp.int32, (SUBLANES, n), 0)
    lane = lax.broadcasted_iota(jnp.int32, (SUBLANES, n), 1)

    def across(value, m):
        return jnp.broadcast_to(value[:, m : m + 1], (SUBLANES, n))

    def down(value, k):
        return jnp.broadcast_to(value[k : k + 1, :], (SUBLANES, n))

    def panel(_, rows):
        head = rows[0]
        split = [across(head, m) for m in range(SUBLANES)]
        for k in range(SUBLANES):
            inverse = 1.0 / down(split[k], k)
            mine = sub == k
            head = jnp.where(lane == k, jnp.where(mine, 1.0, 0.0), head)
            pivot = down(head, k) * inverse
            factor = split[k]
            head = jnp.where(mine, pivot, head - factor * pivot)
            for m in range(k + 1, SUBLANES):
                scaled = down(split[m], k) * inverse
                split[m] = jnp.where(mine, scaled, split[m] - factor * scaled)
        lines = [down(head, m) for m in range(SUBLANES)]
        done = []
        for row in rows[1:]:
            value = jnp.where(lane < SUBLANES, 0.0, row)
            for m in range(SUBLANES):
                value = value - across(row, m) * lines[m]
            done.append(value)
        done.append(head)
        return tuple(pltpu.roll(value, n - SUBLANES, 1) for value in done)

    rows = tuple(matrix[SUBLANES * i : SUBLANES * (i + 1)] for i in range(count))
    rows = lax.fori_loop(0, count, panel, rows)
    return jnp.concatenate(rows, axis=0)


def invert_corner(grid, own_ref, pieces_ref, out_ref, work_ref):
    row_blocks = PANEL // SUB // grid.rows
    col_blocks = PANEL // SUB // grid.cols
    width = col_blocks * SUB
    own_row = own_ref[0] // grid.cols
    own_col = own_ref[0] % grid.cols

    def position(r, b):
        block = r + grid.rows * b
        return pl.multiple_of((((block % grid.cols) ^ own_col) * col_blocks + block // grid.cols) * SUB, SUB)

    for e in range(grid.rows):
        for b in range(row_blocks):
            start = position(own_row ^ e, b)
            for d in range(grid.cols):
                work_ref[pl.ds(start, SUB), d * width : (d + 1) * width] = pieces_ref[
                    d, e, b * SUB : (b + 1) * SUB, :
                ]
    steps = PANEL // LANES
    lane = lax.broadcasted_iota(jnp.int32, (LANES, PANEL), 1) // LANES

    @pl.loop(0, steps)
    def _(step):
        at = pl.ds(pl.multiple_of(step * LANES, LANES), LANES)
        small = invert_block(work_ref[at, at])
        line = jnp.dot(small, work_ref[at, :], precision=highest, preferred_element_type=jnp.float32)
        line = jnp.where(lane == step, jnp.concatenate([small] * steps, axis=1), line)
        for i in range(steps):
            rows = slice(i * LANES, (i + 1) * LANES)
            factor = work_ref[rows, at]
            kept = jnp.where(lane == step, 0.0, work_ref[rows, :])
            update = kept - jnp.dot(
                factor, line, precision=highest, preferred_element_type=jnp.float32
            )
            work_ref[rows, :] = jnp.where(i == step, line, update)

    for i, e in enumerate(grid.order):
        for b in range(row_blocks):
            target = (i * row_blocks + b) * SUB
            out_ref[target : target + SUB, :] = work_ref[pl.ds(position(own_row ^ e, b), SUB), :]


def split(value):
    upper = value.astype(jnp.bfloat16)
    return upper, (value - upper.astype(jnp.float32)).astype(jnp.bfloat16)


def product(left, right):
    total = None
    for i, j in ((0, 1), (1, 0), (0, 0)):
        term = jnp.dot(left[i], right[j], preferred_element_type=jnp.float32)
        total = term if total is None else total + term
    return total


def eliminate_kernel(matrix_ref, solved_ref, *refs):
    parts, out_ref, upper_ref, lower_ref = refs[:-3], refs[-3], refs[-2], refs[-1]

    @pl.when(pl.program_id(0) == 0)
    def _():
        start = 0
        for part in parts:
            rows = slice(start, start + part.shape[0])
            upper_ref[rows, :], lower_ref[rows, :] = split(part[...])
            start += part.shape[0]

    left = split(solved_ref[...])
    width = 256
    for start in range(0, out_ref.shape[1], width):
        at = slice(start, start + width)
        out_ref[:, at] = matrix_ref[:, at] - product(left, (upper_ref[:, at], lower_ref[:, at]))


def eliminate(matrix, solved, parts):
    rows, cols = matrix.shape
    depth = solved.shape[1]
    tile = 256
    return pl.pallas_call(
        eliminate_kernel,
        out_shape=jax.ShapeDtypeStruct((rows, cols), jnp.float32),
        grid=(rows // tile,),
        in_specs=[
            pl.BlockSpec((tile, cols), lambda i: (i, 0)),
            pl.BlockSpec((tile, depth), lambda i: (i, 0)),
        ]
        + [pl.BlockSpec(part.shape, lambda i: (0, 0), pipeline_mode=pl.Buffered(1)) for part in parts],
        out_specs=pl.BlockSpec((tile, cols), lambda i: (i, 0)),
        scratch_shapes=[pltpu.VMEM((depth, cols), jnp.bfloat16)] * 2,
        compiler_params=pltpu.CompilerParams(
            vmem_limit_bytes=VMEM_LIMIT, dimension_semantics=("arbitrary",)
        ),
        cost_estimate=pl.CostEstimate(
            flops=6 * rows * cols * depth, bytes_accessed=12 * rows * cols, transcendentals=0
        ),
    )(matrix, solved, *parts)


def pairs(count, offset):
    return [(i, i ^ offset) for i in range(count)]


def exchange(values, axis, count):
    return [v if d == 0 else lax.ppermute(v, axis, pairs(count, d)) for d, v in enumerate(values)]


def partners(value, axis, count, offsets):
    return [value if d == 0 else lax.ppermute(value, axis, pairs(count, d)) for d in offsets]


def all_rows(value, count):
    both = jnp.stack(partners(value, "row", count, (0, 1)))
    return jnp.concatenate(partners(both, "row", count, range(0, count, 2)))


def line_rows(value, count):
    mine = partners(value, "row", count, range(0, count, 2))
    half = len(mine) // 2
    return jnp.stack(mine[:half]), jnp.stack(mine[half:])


def body(
    inverse_factor,
    coupling,
    boundary_stiffness,
    interior_mass,
    boundary_mass,
    interface_ids,
    trial_modes,
):
    grid = Grid(lax.axis_size("row"), lax.axis_size("col"))
    f32 = jnp.float32
    modes = trial_modes.shape[1]
    mode_count = modes // grid.cols
    per_device = mode_count // SUB
    size = coupling.shape[2]
    local_rows = NG // grid.rows
    local_cols = NG // grid.cols
    runs = interface_ids[:, ::IDB] // IDB
    own = (lax.axis_index("row") * grid.cols + lax.axis_index("col")).astype(jnp.int32).reshape(1)

    factor = inverse_factor[0]
    weighted = jnp.dot(factor, coupling[0], precision=high)
    static = tdot(factor, weighted, high)
    condensed_m = jnp.diag(boundary_mass[0]) + tdot(static, interior_mass[0][:, None] * static, high)
    shifted_s = boundary_stiffness[0] - tdot(weighted, weighted, high) - shift_value * condensed_m

    outbox = call(
        functools.partial(pack_matrix, grid),
        jax.ShapeDtypeStruct((grid.devices, grid.slots, SUBLANES, LANES), f32),
        [SMEM, SMEM, VMEM],
        nbytes=size * size * 8,
    )(runs, own, shifted_s)
    inbox = lax.all_to_all(outbox, ("row", "col"), 0, 0, tiled=True)

    outbox, local_modes, late_runs = lax.optimization_barrier((outbox, trial_modes, runs))
    row_kind = lax.axis_index("row") // PER_RUN
    col_kind = lax.axis_index("col") // PER_RUN
    row_tab = list_places(late_runs, grid.row_classes, row_kind, grid.row_cap)
    col_tab = list_places(late_runs, grid.col_classes, col_kind, grid.col_cap)
    wanted = call(
        functools.partial(pick_modes, grid),
        jax.ShapeDtypeStruct((grid.cols, grid.col_cap, SUB, modes), f32),
        [SMEM, SMEM, VMEM],
        nbytes=trial_modes.size * 8,
    )(runs, own, local_modes)
    wanted = jnp.stack(exchange([wanted[d] for d in range(grid.cols)], "col", grid.cols))
    own_modes = call(
        functools.partial(order_modes, grid),
        jax.ShapeDtypeStruct((size, modes), f32),
        [SMEM, SMEM, VMEM],
        nbytes=size * modes * 8,
    )(runs, own, wanted)
    weighted_modes = tdot(own_modes, condensed_m, high)
    mode_outbox = call(
        functools.partial(pack_modes, grid, per_device),
        jax.ShapeDtypeStruct((grid.devices, grid.row_cap * per_device, SUBLANES, LANES), f32),
        [SMEM, SMEM, VMEM],
        nbytes=size * modes * 8,
    )(runs, own, weighted_modes)

    inbox, mode_outbox = lax.optimization_barrier((inbox, mode_outbox))
    panel_row_count = PANEL // grid.rows
    panel_col_count = PANEL // grid.cols
    row_part, col_part, corner = call(
        functools.partial(place_panel, grid),
        (
            jax.ShapeDtypeStruct((panel_row_count, local_cols), f32),
            jax.ShapeDtypeStruct((local_rows, panel_col_count), f32),
            jax.ShapeDtypeStruct((panel_row_count, panel_col_count), f32),
        ),
        [SMEM, SMEM, VMEM],
        nbytes=size * size * 4,
    )(row_tab, col_tab, inbox)

    pieces = all_rows(corner, grid.rows)
    pieces, row_part, col_part, mode_outbox, inbox = lax.optimization_barrier(
        (pieces, row_part, col_part, mode_outbox, inbox)
    )
    pieces = jnp.stack(partners(pieces, "col", grid.cols, range(grid.cols)))
    line = line_rows(row_part, grid.rows)
    shifted = call(
        functools.partial(place_matrix, grid),
        jax.ShapeDtypeStruct((local_rows, local_cols), f32),
        [SMEM, SMEM, VMEM],
        nbytes=local_rows * local_cols * 8,
    )(row_tab, col_tab, inbox)
    pieces, col_part, mode_outbox, shifted = lax.optimization_barrier(
        (pieces, col_part, mode_outbox, shifted)
    )
    panel_cols = jnp.concatenate(partners(col_part, "col", grid.cols, range(grid.cols)), axis=1)
    mode_inbox = lax.all_to_all(mode_outbox, ("row", "col"), 0, 0, tiled=True)
    inverse = call(
        functools.partial(invert_corner, grid),
        jax.ShapeDtypeStruct((PANEL, PANEL), f32),
        [SMEM, VMEM],
        [pltpu.VMEM((PANEL, PANEL), f32)],
        flops=4 * PANEL**3,
        nbytes=PANEL * PANEL * 80,
    )(own, pieces)
    solved = lax.dot_general(panel_cols, inverse, (((1,), (1,)), ((), ())), precision=highest)
    solved, line = lax.optimization_barrier((solved, line))
    panel_rows = []
    for part in line:
        for stack in partners(part, "row", grid.rows, (0, 1)):
            panel_rows.append(stack.reshape(-1, local_cols))
    solved, mode_inbox = lax.optimization_barrier((solved, mode_inbox))
    modes_local = call(
        functools.partial(place_modes, grid, per_device),
        jax.ShapeDtypeStruct((mode_count, local_rows), f32),
        [SMEM, VMEM],
        nbytes=mode_count * local_rows * 8,
    )(row_tab, mode_inbox)
    panel_modes = modes_local[:, :panel_row_count].T
    panel_modes = jnp.stack(partners(panel_modes, "row", grid.rows, (0, 1)))
    panel_modes, shifted = lax.optimization_barrier((panel_modes, shifted))
    panel_modes = partners(panel_modes, "row", grid.rows, range(0, grid.rows, 2))
    reduced_matrix = eliminate(shifted, solved, panel_rows)
    panel_modes = jnp.concatenate(panel_modes)
    panel_modes = jnp.concatenate([panel_modes[e] for e in grid.order])
    reduced_columns = modes_local - lax.dot_general(
        panel_modes, solved, (((0,), (1,)), ((), ())), precision=high
    )
    return (reduced_matrix, reduced_columns)


def solution(mesh):
    return jax.shard_map(
        body,
        mesh=mesh,
        in_specs=(
            P(("row", "col"), None, None),
            P(("row", "col"), None, None),
            P(("row", "col"), None, None),
            P(("row", "col"), None),
            P(("row", "col"), None),
            P(),
            P("col", None),
        ),
        out_specs=(P("row", "col"), P("col", "row")),
        check_vma=False,
    )
```

```python
import functools
import jax
import jax.numpy as jnp
from jax import lax
from jax.experimental import pallas as pl
from jax.experimental.pallas import tpu as pltpu
from jax.sharding import PartitionSpec as P

IDB = 128
SUB = 32
NG = 8192
PANEL = 512
PER_RUN = IDB // SUB
LANES = 128
SUBLANES = 8
GROUPS = SUB // SUBLANES

highest = lax.Precision.HIGHEST
high = lax.Precision.HIGH
shift_value = 0.05
MIB = 1024 * 1024


def tdot(left, right, precision):
    return lax.dot_general(left, right, (((0,), (0,)), ((), ())), precision=precision)


class Grid:
    def __init__(self, row_count, col_count):
        self.rows = row_count
        self.cols = col_count
        self.devices = row_count * col_count
        self.row_classes = row_count // PER_RUN
        self.col_classes = col_count // PER_RUN
        self.row_cap = 3
        self.col_cap = 3 + (self.row_classes // self.col_classes - 1) * (3 // (self.row_classes - 1))
        self.slots = self.row_cap * self.col_cap


def call(kernel, out_shape, in_specs, scratch=(), flops=0, nbytes=0, limit=20):
    return pl.pallas_call(
        kernel,
        out_shape=out_shape,
        in_specs=in_specs,
        out_specs=jax.tree.map(lambda _: pl.BlockSpec(memory_space=pltpu.VMEM), out_shape),
        scratch_shapes=list(scratch),
        compiler_params=pltpu.CompilerParams(vmem_limit_bytes=limit * MIB),
        cost_estimate=pl.CostEstimate(flops=flops, bytes_accessed=nbytes, transcendentals=0),
    )


SMEM = pl.BlockSpec(memory_space=pltpu.SMEM)
VMEM = pl.BlockSpec(memory_space=pltpu.VMEM)


def ranks_of(groups, classes):
    kinds = [g % classes for g in groups]
    ranks = []
    for j in range(len(kinds)):
        rank = jnp.int32(0)
        for i in range(j):
            rank = rank + jnp.where(kinds[i] == kinds[j], 1, 0).astype(jnp.int32)
        ranks.append(rank)
    return kinds, ranks


def lane_group():
    return lax.broadcasted_iota(jnp.int32, (SUBLANES, LANES), 1) // SUB


def regroup(ref, row, lanes, turn):
    parts = []
    for g in range(GROUPS):
        start = row + (g - turn + GROUPS) % GROUPS * SUBLANES
        parts.append(ref[pl.ds(pl.multiple_of(start, SUBLANES), SUBLANES), lanes])
    where = lane_group()
    out = []
    for k in range(PER_RUN):
        value = None
        for g in range(GROUPS):
            shift = (g - k) % PER_RUN * SUB
            piece = parts[g] if shift == 0 else pltpu.roll(parts[g], shift, 1)
            value = piece if value is None else jnp.where(where == g, piece, value)
        out.append(value)
    return out


def pack_matrix(grid, runs_ref, own_ref, a_ref, out_ref):
    number = a_ref.shape[0] // IDB
    groups = [runs_ref[own_ref[0], j] for j in range(number)]
    row_kind, row_rank = ranks_of(groups, grid.row_classes)
    col_kind, col_rank = ranks_of(groups, grid.col_classes)
    turn = [g // grid.col_classes % PER_RUN for g in groups]
    if grid.devices * grid.slots != (number * PER_RUN) ** 2:
        out_ref[...] = jnp.zeros_like(out_ref)
    for i in range(number):
        for k in range(PER_RUN):
            for j in range(number):
                lanes = slice(j * IDB, (j + 1) * IDB)
                row = (row_kind[i] * PER_RUN + k) * grid.cols
                slot = row_rank[i] * grid.col_cap + col_rank[j]
                for kk, value in enumerate(regroup(a_ref, i * IDB + k * SUB, lanes, turn[j])):
                    out_ref[row + col_kind[j] * PER_RUN + kk, slot] = value


def pack_modes(grid, per_device, runs_ref, own_ref, y_ref, out_ref):
    number = y_ref.shape[1] // IDB
    groups = [runs_ref[own_ref[0], j] for j in range(number)]
    row_kind, row_rank = ranks_of(groups, grid.row_classes)
    turn = [g // grid.row_classes % PER_RUN for g in groups]
    if grid.devices * grid.row_cap != number * PER_RUN * grid.cols:
        out_ref[...] = jnp.zeros_like(out_ref)
    for m in range(y_ref.shape[0] // SUB):
        for j in range(number):
            lanes = slice(j * IDB, (j + 1) * IDB)
            slot = row_rank[j] * per_device + m % per_device
            for k, value in enumerate(regroup(y_ref, m * SUB, lanes, turn[j])):
                row = (row_kind[j] * PER_RUN + k) * grid.cols + m // per_device
                out_ref[row, slot] = value


def list_places(runs, classes, kind, cap):
    mine = (runs % classes == kind).astype(jnp.int32)
    number = runs.shape[1]
    earlier = jnp.arange(number)[:, None] < jnp.arange(number)[None, :]
    rank = jnp.sum(jnp.where(earlier[None], mine[:, :, None], 0), axis=1)
    hit = (mine[:, :, None] == 1) & (rank[:, :, None] == jnp.arange(cap)[None, None, :])
    return jnp.sum(jnp.where(hit, runs[:, :, None] // classes + 1, 0), axis=1) - 1


def add_blocks(acc_ref, blocks):
    where = lane_group()
    todo = []
    for row, place, value in blocks:
        valid = place >= 0
        place = jnp.maximum(place, 0)
        start = pl.multiple_of(place // PER_RUN * LANES, LANES)
        mask = (where == place % PER_RUN) & valid
        for q in range(GROUPS):
            moved = value if q == 0 else pltpu.roll(value, LANES - q * SUB, 1)
            at = (pl.ds(row + q * SUBLANES, SUBLANES), pl.ds(start, LANES))
            todo.append((at, acc_ref[at] + moved, mask))
    for at, value, mask in todo:
        pltpu.store(acc_ref.at[at], value, mask=mask)


def place_matrix(grid, row_tab, col_tab, in_ref, acc_ref):
    acc_ref[...] = jnp.zeros_like(acc_ref)

    @pl.loop(0, row_tab.shape[0])
    def _(s):
        blocks = []
        for t in range(grid.row_cap):
            row_place = row_tab[s, t]
            row = pl.multiple_of(jnp.maximum(row_place, 0) * SUB, SUB)
            for u in range(grid.col_cap):
                place = jnp.where(row_place >= 0, col_tab[s, u], -1)
                blocks.append((row, place, in_ref[s, t * grid.col_cap + u]))
        add_blocks(acc_ref, blocks)


def place_panel(grid, row_tab, col_tab, in_ref, rows_ref, cols_ref, corner_ref):
    row_limit = rows_ref.shape[0] // SUB
    col_limit = cols_ref.shape[1] // SUB
    rows_ref[...] = jnp.zeros_like(rows_ref)
    cols_ref[...] = jnp.zeros_like(cols_ref)

    @pl.loop(0, row_tab.shape[0])
    def _(s):
        def row_of(t):
            return pl.multiple_of(jnp.maximum(row_tab[s, t], 0) * SUB, SUB)

        for t in range(grid.row_cap):

            @pl.when((row_tab[s, t] >= 0) & (row_tab[s, t] < row_limit))
            def _():
                add_blocks(
                    rows_ref,
                    [(row_of(t), col_tab[s, u], in_ref[s, t * grid.col_cap + u]) for u in range(grid.col_cap)],
                )

        for u in range(grid.col_cap):

            @pl.when((col_tab[s, u] >= 0) & (col_tab[s, u] < col_limit))
            def _():
                add_blocks(
                    cols_ref,
                    [
                        (row_of(t), jnp.where(row_tab[s, t] >= 0, col_tab[s, u], -1), in_ref[s, t * grid.col_cap + u])
                        for t in range(grid.row_cap)
                    ],
                )

    corner_ref[...] = cols_ref[: row_limit * SUB, : col_limit * SUB]


def place_modes(grid, per_device, row_tab, in_ref, acc_ref):
    acc_ref[...] = jnp.zeros_like(acc_ref)

    @pl.loop(0, row_tab.shape[0])
    def _(s):
        blocks = []
        for t in range(grid.row_cap):
            place = row_tab[s, t]
            blocks += [(m * SUB, place, in_ref[s, t * per_device + m]) for m in range(per_device)]
        add_blocks(acc_ref, blocks)


def pick_modes(grid, runs_ref, own_ref, modes_ref, out_ref):
    number = runs_ref.shape[1]
    own_row = own_ref[0] // grid.cols
    own_col = own_ref[0] % grid.cols
    col_kind = own_col // PER_RUN
    if grid.cols * grid.col_cap != number * PER_RUN:
        out_ref[...] = jnp.zeros_like(out_ref)
    for c in range(grid.cols):
        groups = [runs_ref[own_row * grid.cols + (own_col ^ c), j] for j in range(number)]
        kinds, ranks = ranks_of(groups, grid.col_classes)
        for j in range(number):

            @pl.when(kinds[j] == col_kind)
            def _():
                row = pl.multiple_of(groups[j] // grid.col_classes * SUB, SUB)
                out_ref[c, ranks[j]] = modes_ref[pl.ds(row, SUB), :]


def order_modes(grid, runs_ref, own_ref, in_ref, out_ref):
    own_col = own_ref[0] % grid.cols
    number = runs_ref.shape[1]
    groups = [runs_ref[own_ref[0], j] for j in range(number)]
    kinds, ranks = ranks_of(groups, grid.col_classes)
    for j in range(number):
        for k in range(PER_RUN):
            start = j * IDB + k * SUB
            out_ref[start : start + SUB, :] = in_ref[(kinds[j] * PER_RUN + k) ^ own_col, ranks[j]]


def invert_block(matrix):
    n = matrix.shape[0]
    count = n // SUBLANES
    sub = lax.broadcasted_iota(jnp.int32, (SUBLANES, n), 0)
    lane = lax.broadcasted_iota(jnp.int32, (SUBLANES, n), 1)

    def across(value, m):
        return jnp.broadcast_to(value[:, m : m + 1], (SUBLANES, n))

    def down(value, k):
        return jnp.broadcast_to(value[k : k + 1, :], (SUBLANES, n))

    def panel(_, rows):
        head = rows[0]
        split = [across(head, m) for m in range(SUBLANES)]
        for k in range(SUBLANES):
            inverse = 1.0 / down(split[k], k)
            mine = sub == k
            head = jnp.where(lane == k, jnp.where(mine, 1.0, 0.0), head)
            pivot = down(head, k) * inverse
            factor = split[k]
            head = jnp.where(mine, pivot, head - factor * pivot)
            for m in range(k + 1, SUBLANES):
                scaled = down(split[m], k) * inverse
                split[m] = jnp.where(mine, scaled, split[m] - factor * scaled)
        lines = [down(head, m) for m in range(SUBLANES)]
        done = []
        for row in rows[1:]:
            value = jnp.where(lane < SUBLANES, 0.0, row)
            for m in range(SUBLANES):
                value = value - across(row, m) * lines[m]
            done.append(value)
        done.append(head)
        return tuple(pltpu.roll(value, n - SUBLANES, 1) for value in done)

    rows = tuple(matrix[SUBLANES * i : SUBLANES * (i + 1)] for i in range(count))
    rows = lax.fori_loop(0, count, panel, rows)
    return jnp.concatenate(rows, axis=0)


def invert_corner(grid, own_ref, pieces_ref, out_ref, work_ref):
    row_blocks = PANEL // SUB // grid.rows
    col_blocks = PANEL // SUB // grid.cols
    width = col_blocks * SUB
    own_row = own_ref[0] // grid.cols
    own_col = own_ref[0] % grid.cols

    def position(r, b):
        block = r + grid.rows * b
        return pl.multiple_of((((block % grid.cols) ^ own_col) * col_blocks + block // grid.cols) * SUB, SUB)

    for e in range(grid.rows):
        for b in range(row_blocks):
            start = position(own_row ^ e, b)
            for d in range(grid.cols):
                work_ref[pl.ds(start, SUB), d * width : (d + 1) * width] = pieces_ref[
                    d, e, b * SUB : (b + 1) * SUB, :
                ]
    steps = PANEL // LANES
    lane = lax.broadcasted_iota(jnp.int32, (LANES, PANEL), 1) // LANES

    @pl.loop(0, steps)
    def _(step):
        at = pl.ds(pl.multiple_of(step * LANES, LANES), LANES)
        small = invert_block(work_ref[at, at])
        line = jnp.dot(small, work_ref[at, :], precision=highest, preferred_element_type=jnp.float32)
        line = jnp.where(lane == step, jnp.concatenate([small] * steps, axis=1), line)
        for i in range(steps):
            rows = slice(i * LANES, (i + 1) * LANES)
            factor = work_ref[rows, at]
            kept = jnp.where(lane == step, 0.0, work_ref[rows, :])
            update = kept - jnp.dot(
                factor, line, precision=highest, preferred_element_type=jnp.float32
            )
            work_ref[rows, :] = jnp.where(i == step, line, update)

    for e in range(grid.rows):
        for b in range(row_blocks):
            target = (e * row_blocks + b) * SUB
            out_ref[target : target + SUB, :] = work_ref[pl.ds(position(own_row ^ e, b), SUB), :]


def split(value):
    upper = value.astype(jnp.bfloat16)
    return upper, (value - upper.astype(jnp.float32)).astype(jnp.bfloat16)


def product(left, right):
    total = None
    for i, j in ((0, 1), (1, 0), (0, 0)):
        term = jnp.dot(left[i], right[j], preferred_element_type=jnp.float32)
        total = term if total is None else total + term
    return total


def eliminate_kernel(skip, matrix_ref, solved_ref, *refs):
    parts, out_ref, upper_ref, lower_ref = refs[skip:-3], refs[-3], refs[-2], refs[-1]

    @pl.when(pl.program_id(0) == 0)
    def _():
        start = 0
        for part in parts:
            rows = slice(start, start + part.shape[0])
            upper_ref[rows, :], lower_ref[rows, :] = split(part[...])
            start += part.shape[0]

    left = split(solved_ref[...])
    width = 256
    for start in range(0, out_ref.shape[1], width):
        at = slice(start, start + width)
        out_ref[:, at] = matrix_ref[:, at] - product(left, (upper_ref[:, at], lower_ref[:, at]))


def eliminate(matrix, solved, parts, half, into=()):
    rows, cols = matrix.shape
    depth = solved.shape[1]
    tile = 256 if rows % 512 == 0 else rows // 2
    tiles = rows // 2 // tile
    first = half * tiles
    return pl.pallas_call(
        functools.partial(eliminate_kernel, len(into)),
        out_shape=jax.ShapeDtypeStruct((rows, cols), jnp.float32),
        grid=(tiles,),
        in_specs=[
            pl.BlockSpec((tile, cols), lambda i: (i + first, 0)),
            pl.BlockSpec((tile, depth), lambda i: (i + first, 0)),
        ]
        + [pl.BlockSpec(memory_space=pl.ANY) for _ in into]
        + [pl.BlockSpec(part.shape, lambda i: (0, 0), pipeline_mode=pl.Buffered(1)) for part in parts],
        out_specs=pl.BlockSpec((tile, cols), lambda i: (i + first, 0)),
        scratch_shapes=[pltpu.VMEM((depth, cols), jnp.bfloat16)] * 2,
        input_output_aliases={2: 0} if into else {},
        compiler_params=pltpu.CompilerParams(
            vmem_limit_bytes=32 * MIB, dimension_semantics=("arbitrary",)
        ),
        cost_estimate=pl.CostEstimate(
            flops=3 * rows * cols * depth, bytes_accessed=6 * rows * cols, transcendentals=0
        ),
    )(matrix, solved, *into, *parts)


def pairs(count, offset):
    return [(i, i ^ offset) for i in range(count)]


def exchange(values, axis, count):
    return [v if d == 0 else lax.ppermute(v, axis, pairs(count, d)) for d, v in enumerate(values)]


def partners(value, axis, count, offsets):
    return [value if d == 0 else lax.ppermute(value, axis, pairs(count, d)) for d in offsets]


def body(
    inverse_factor,
    coupling,
    boundary_stiffness,
    interior_mass,
    boundary_mass,
    interface_ids,
    trial_modes,
):
    grid = Grid(lax.axis_size("row"), lax.axis_size("col"))
    f32 = jnp.float32
    modes = trial_modes.shape[1]
    mode_count = modes // grid.cols
    per_device = mode_count // SUB
    size = coupling.shape[2]
    local_rows = NG // grid.rows
    local_cols = NG // grid.cols
    runs = interface_ids[:, ::IDB] // IDB
    own = (lax.axis_index("row") * grid.cols + lax.axis_index("col")).astype(jnp.int32).reshape(1)

    factor = inverse_factor[0]
    weighted = jnp.dot(factor, coupling[0], precision=high)
    static = tdot(factor, weighted, high)
    condensed_m = jnp.diag(boundary_mass[0]) + tdot(static, interior_mass[0][:, None] * static, high)
    shifted_s = boundary_stiffness[0] - tdot(weighted, weighted, high) - shift_value * condensed_m

    outbox = call(
        functools.partial(pack_matrix, grid),
        jax.ShapeDtypeStruct((grid.devices, grid.slots, SUBLANES, LANES), f32),
        [SMEM, SMEM, VMEM],
        nbytes=size * size * 8,
    )(runs, own, shifted_s)
    inbox = lax.all_to_all(outbox, ("row", "col"), 0, 0, tiled=True)

    outbox, local_modes, late_runs = lax.optimization_barrier((outbox, trial_modes, runs))
    row_kind = lax.axis_index("row") // PER_RUN
    col_kind = lax.axis_index("col") // PER_RUN
    row_tab = list_places(late_runs, grid.row_classes, row_kind, grid.row_cap)
    col_tab = list_places(late_runs, grid.col_classes, col_kind, grid.col_cap)
    wanted = call(
        functools.partial(pick_modes, grid),
        jax.ShapeDtypeStruct((grid.cols, grid.col_cap, SUB, modes), f32),
        [SMEM, SMEM, VMEM],
        nbytes=trial_modes.size * 8,
    )(runs, own, local_modes)
    wanted = jnp.stack(exchange([wanted[d] for d in range(grid.cols)], "col", grid.cols))
    own_modes = call(
        functools.partial(order_modes, grid),
        jax.ShapeDtypeStruct((size, modes), f32),
        [SMEM, SMEM, VMEM],
        nbytes=size * modes * 8,
    )(runs, own, wanted)
    weighted_modes = tdot(own_modes, condensed_m, high)
    inbox, weighted_modes = lax.optimization_barrier((inbox, weighted_modes))
    mode_outbox = call(
        functools.partial(pack_modes, grid, per_device),
        jax.ShapeDtypeStruct((grid.devices, grid.row_cap * per_device, SUBLANES, LANES), f32),
        [SMEM, SMEM, VMEM],
        nbytes=size * modes * 8,
    )(runs, own, weighted_modes)
    panel_row_count = PANEL // grid.rows
    panel_col_count = PANEL // grid.cols
    row_part, col_part, corner = call(
        functools.partial(place_panel, grid),
        (
            jax.ShapeDtypeStruct((panel_row_count, local_cols), f32),
            jax.ShapeDtypeStruct((local_rows, panel_col_count), f32),
            jax.ShapeDtypeStruct((panel_row_count, panel_col_count), f32),
        ),
        [SMEM, SMEM, VMEM],
        nbytes=size * size * 4,
    )(row_tab, col_tab, inbox)

    pieces = jnp.stack(partners(corner, "row", grid.rows, (0, 1)))
    pieces = jnp.concatenate(partners(pieces, "row", grid.rows, range(0, grid.rows, 2)))
    pieces, row_part, col_part, mode_outbox, inbox = lax.optimization_barrier(
        (pieces, row_part, col_part, mode_outbox, inbox)
    )
    pieces = jnp.stack(partners(pieces, "col", grid.cols, range(grid.cols)))
    line = partners(row_part, "row", grid.rows, [1, *range(2, grid.rows, 2)])
    shifted = call(
        functools.partial(place_matrix, grid),
        jax.ShapeDtypeStruct((local_rows, local_cols), f32),
        [SMEM, SMEM, VMEM],
        nbytes=local_rows * local_cols * 8,
    )(row_tab, col_tab, inbox)
    pieces, col_part, mode_outbox, shifted = lax.optimization_barrier(
        (pieces, col_part, mode_outbox, shifted)
    )
    panel_cols = jnp.concatenate(partners(col_part, "col", grid.cols, range(grid.cols)), axis=1)
    mode_inbox = lax.all_to_all(mode_outbox, ("row", "col"), 0, 0, tiled=True)
    inverse = call(
        functools.partial(invert_corner, grid),
        jax.ShapeDtypeStruct((PANEL, PANEL), f32),
        [SMEM, VMEM],
        [pltpu.VMEM((PANEL, PANEL), f32)],
        flops=4 * PANEL**3,
        nbytes=PANEL * PANEL * 80,
    )(own, pieces)
    inverse, rest = lax.optimization_barrier((inverse, line[1:]))
    solved = lax.dot_general(panel_cols, inverse, (((1,), (1,)), ((), ())), precision=highest)
    panel_rows = [row_part, line[0]]
    for part in rest:
        panel_rows += partners(part, "row", grid.rows, (0, 1))
    reduced_matrix = eliminate(shifted, solved, panel_rows, 0)
    modes_local = call(
        functools.partial(place_modes, grid, per_device),
        jax.ShapeDtypeStruct((mode_count, local_rows), f32),
        [SMEM, VMEM],
        nbytes=mode_count * local_rows * 8,
    )(row_tab, mode_inbox)
    panel_modes = modes_local[:, :panel_row_count].T
    panel_modes = jnp.stack(partners(panel_modes, "row", grid.rows, (0, 1)))
    panel_modes, reduced_matrix = lax.optimization_barrier((panel_modes, reduced_matrix))
    panel_modes = partners(panel_modes, "row", grid.rows, range(0, grid.rows, 2))
    reduced_matrix = eliminate(shifted, solved, panel_rows, 1, (reduced_matrix,))
    panel_modes = jnp.concatenate(panel_modes).reshape(PANEL, -1)
    reduced_columns = modes_local - lax.dot_general(
        panel_modes, solved, (((0,), (1,)), ((), ())), precision=high
    )
    return (reduced_matrix, reduced_columns)


def solution(mesh):
    return jax.shard_map(
        body,
        mesh=mesh,
        in_specs=(
            P(("row", "col"), None, None),
            P(("row", "col"), None, None),
            P(("row", "col"), None, None),
            P(("row", "col"), None),
            P(("row", "col"), None),
            P(),
            P("col", None),
        ),
        out_specs=(P("row", "col"), P("col", "row")),
        check_vma=False,
    )
```
